32 devices in a mesh: atom: 16 (over z, y, x), wave: 2 (over core).
Axes of the slice: x: 2, y: 2, z: 4, core: 2. Of those that a mesh axis runs over, the one named last changes fastest.
Arguments:
- positions: float32 [3, 4096], P(None, ('atom', 'wave')), may hold values from 0 to 1
- counts: int32 [32], P(('atom', 'wave')), may hold values from 16 to 128, as said below
- feats: bfloat16 [4096, 256], P(('atom', 'wave')), may hold values from -6 to 6
- waves: int32 [3, 8192], P(None, 'wave'), may hold values from -12 to 12
- wave_filter: bfloat16 [8192, 256], P('wave'), may hold values from -5 to 5
- mixing: float32 [256, 256], replicated, may hold values from -0.375 to 0.375
- gain: float32 [256], replicated, may hold values from 0.1 to 1.9
- w_in: bfloat16 [256, 1024], replicated, may hold values from -0.375 to 0.375
- w_out: bfloat16 [1024, 256], replicated, may hold values from -0.1875 to 0.1875
Outputs:
- updated: bfloat16 [4096, 256], P(('atom', 'wave'))
The draws below stay inside these ranges and needn't reach their ends.
Inputs may be any that keep to these rules, and one draw needn't show every extreme that they name: `counts`: each block of 128 slots holds 16 to 128 live atoms at its start; every even-numbered block is full.
All inputs are finite; a program needn't handle non-finite values.
Results may differ from the reference program's by a relative error of at most 0.0055.
Values may be sent and summed in bfloat16 or wider, within the bound.
A program may use at most 128 MiB of HBM per device.

```python
import math
import jax
import jax.numpy as jnp
from jax import lax

C = 256
HID = 1024
KWAVES = 8192
ATOMS = 4096
BLOCKS = 32


def draw_counts(key, part):
    values = jax.random.randint(jax.random.fold_in(key, 11), (BLOCKS,), 16, 129)
    index = jnp.arange(BLOCKS, dtype=jnp.int32)
    return jnp.where(index % 2 == 0, 128, values).astype(jnp.int32)


def set_ends(drawn, rng, least, top_value):
    shape = drawn.shape
    place = [jax.random.randint(jax.random.fold_in(rng, axis), (), 0, shape[axis]) for axis in range(len(shape))]
    drawn = drawn.at[tuple(place)].set(least)
    longest = shape.index(max(shape))
    place[longest] = (place[longest] + 1) % shape[longest]
    return drawn.at[tuple(place)].set(top_value)


def levels(rng, shape, split, low, high):
    level, own = 1.0, jax.random.fold_in(rng, 6)
    for axis_at, parts in split:
        steps = jnp.exp(jax.random.uniform(jax.random.fold_in(own, axis_at), (parts,), jnp.float32, low / len(split), high / len(split)))
        level = level * jnp.repeat(steps, shape[axis_at] // parts).reshape([-1 if axis == axis_at else 1 for axis in range(len(shape))])
    return level


def normal_values(stream_key, extent, deviation, limit, split=(), kind=jnp.bfloat16):
    level = levels(stream_key, extent, split, -0.22, 0.18) if split else 1.0
    drawn = jax.random.normal(stream_key, extent, jnp.float32) * deviation * level
    return jnp.minimum(jnp.maximum(drawn, -limit), limit).astype(kind)


def setup_inputs(seed: int = 0) -> dict:
    seeds = jax.random.split(jax.random.key(seed), 10)
    positions = jnp.clip(1.0 * jax.random.uniform(seeds[0], (3, ATOMS), jnp.float32) ** levels(seeds[0], (3, ATOMS), ((1, 32),), -0.2, 0.2), 0.0, 1.0)
    counts = draw_counts(jax.random.fold_in(seeds[9], 71), 0)
    feats = normal_values(seeds[2], (ATOMS, C), 1.0, 6.0, ((0, 32),))
    waves = set_ends(jax.random.randint(seeds[3], (3, KWAVES), -12, 13), jax.random.fold_in(seeds[3], 1), -12, 12).astype(jnp.int32)
    wave_filter = normal_values(seeds[4], (KWAVES, C), 1.0, 5.0, ((0, 2),))
    mixing = normal_values(seeds[5], (C, C), C ** -0.5, 0.375, (), jnp.float32)
    gain = jnp.clip(1.0 + 0.18 * jax.random.normal(seeds[6], (C,), jnp.float32), 0.1, 1.9)
    w_in = normal_values(seeds[7], (C, HID), C ** -0.5, 0.375)
    w_out = normal_values(seeds[8], (HID, C), HID ** -0.5, 0.1875)
    return dict(positions=positions, counts=counts, feats=feats, waves=waves, wave_filter=wave_filter, mixing=mixing, gain=gain, w_in=w_in, w_out=w_out)


two_pi = 2.0 * math.pi

def phases(coords, wave_f):
    return (coords[0][:, None] * wave_f[0][None, :] + coords[1][:, None] * wave_f[1][None, :] + coords[2][:, None] * wave_f[2][None, :]) * two_pi

def reference(positions, counts, feats, waves, wave_filter, mixing, gain, w_in, w_out):
    slot = lax.broadcasted_iota(jnp.int32, (BLOCKS, 128), 1)
    live = (slot < counts[:, None]).reshape(ATOMS)
    masked = feats * live[:, None].astype(jnp.bfloat16)
    wave_f = waves.astype(jnp.float32)
    size = 512 if ATOMS % 512 == 0 else 128
    steps_n = ATOMS // size

    def forward(carry, index):
        start = (index * size).astype(jnp.int32)
        coords = lax.dynamic_slice_in_dim(positions, start, size, 1)
        rows_h = lax.dynamic_slice_in_dim(masked, start, size, 0)
        angle = phases(coords, wave_f)
        cosine = jnp.cos(angle).astype(jnp.bfloat16)
        sine = jnp.sin(angle).astype(jnp.bfloat16)
        real_add = jnp.dot(cosine.T, rows_h, preferred_element_type=jnp.float32)
        imag_add = jnp.dot(sine.T, rows_h, preferred_element_type=jnp.float32)
        return ((carry[0] + real_add, carry[1] + imag_add), None)
    zero = jnp.zeros((KWAVES, C), jnp.float32)
    (real_sum, imag_sum), _ = lax.scan(forward, (zero, zero), jnp.arange(steps_n, dtype=jnp.int32))
    scale = 1.0 / math.sqrt(ATOMS)
    filt = wave_filter.astype(jnp.float32)
    filtered_real = jnp.dot(real_sum * scale * filt, mixing, precision=lax.Precision.HIGHEST).astype(jnp.bfloat16)
    filtered_imag = jnp.dot(imag_sum * scale * filt, mixing, precision=lax.Precision.HIGHEST).astype(jnp.bfloat16)
    inv_k = 1.0 / math.sqrt(KWAVES)

    def inverse(index):
        start = (index * size).astype(jnp.int32)
        coords = lax.dynamic_slice_in_dim(positions, start, size, 1)
        angle = phases(coords, wave_f)
        cosine = jnp.cos(angle).astype(jnp.bfloat16)
        sine = jnp.sin(angle).astype(jnp.bfloat16)
        field = jnp.dot(cosine, filtered_real, preferred_element_type=jnp.float32) + jnp.dot(sine, filtered_imag, preferred_element_type=jnp.float32)
        return field * inv_k
    update = lax.map(inverse, jnp.arange(steps_n, dtype=jnp.int32)).reshape(ATOMS, C)
    state = feats.astype(jnp.float32) + update
    meansq = lax.optimization_barrier(jnp.mean(state * state, axis=1, keepdims=True))
    normed = (state * lax.rsqrt(meansq + 1e-06) * gain[None, :]).astype(jnp.bfloat16)
    hidden = jax.nn.silu(jnp.dot(normed, w_in, preferred_element_type=jnp.float32)).astype(jnp.bfloat16)
    result = state + jnp.dot(hidden, w_out, preferred_element_type=jnp.float32)
    return jnp.where(live[:, None], result, 0.0).astype(jnp.bfloat16)
```

```python
import functools
import math

import jax
import jax.numpy as jnp
from jax import lax
from jax.experimental import pallas as pl
from jax.experimental.pallas import tpu as pltpu
from jax.sharding import PartitionSpec as P

MESH = pl.DeviceIdType.MESH
BF, F32 = jnp.bfloat16, jnp.float32
HIGHEST = lax.Precision.HIGHEST
SIN = (4.442883014678955, -7.308245658874512, 3.606354236602783, -0.8461116552352905, 0.1098245158791542)
COS = (1.4142135381698608, -6.978850841522217, 5.739460468292236, -1.883557915687561, 0.3106880187988281)


def horner(z, coefs):
    total = coefs[-1]
    for value in coefs[-2::-1]:
        total = total * z + value
    return total


def grid_of(n):
    side = 1
    while n % (4 * side * side) == 0 and 8 * side**3 <= n:
        side *= 2
    return n // (side * side), side


def kernel(
    n,
    planes,
    side,
    atoms_all,
    kwaves_all,
    counts_ref,
    pos_ref,
    masked_ref,
    wave_ref,
    filt_ref,
    mixing_ref,
    gain_ref,
    w_in_ref,
    w_out_ref,
    out_ref,
    pos_all,
    feat_all,
    wave_other,
    trig,
    factors,
    factors_in,
    field_t,
    field_other,
    kept,
    send_u,
    recv_u,
    p_send,
    p_recv,
    f_send,
    f_recv,
    u_send,
    u_recv,
    c_send,
    c_recv,
):
    kw = wave_ref.shape[0]
    rows, width = masked_ref.shape
    me = lax.axis_index("atom")
    core = lax.axis_index("wave")
    x = me % side
    y = (me // side) % side
    z = me // (side * side)
    b = y + core * (x - y)
    c = x + core * (y - x)
    stride_b = side + core * (1 - side)
    stride_c = 1 + core * (side - 1)

    def at(zz, bb, cc):
        return (zz * (side * side) + bb * stride_b + cc * stride_c, core)

    def ident(dz, db, dc):
        return (dc * side + db) * planes + dz

    partner = (me, 1 - core)
    ahead = (
        [at((z + d) % planes, b, c) for d in range(1, planes)],
        [at(z, (b + d) % side, c) for d in range(1, side)],
        [at(z, b, (c + d) % side) for d in range(1, side)],
    )
    back = (
        [at((z + planes - d) % planes, b, c) for d in range(1, planes)],
        [at(z, (b + side - d) % side, c) for d in range(1, side)],
        [at(z, b, (c + side - d) % side) for d in range(1, side)],
    )

    barrier = pltpu.get_barrier_semaphore()
    peers = [partner] + [peer for group in ahead for peer in group]
    for peer in peers:
        pl.semaphore_signal(barrier, inc=1, device_id=peer, device_id_type=MESH)
    pl.semaphore_wait(barrier, len(peers))

    def gather(own, store, send, recv):
        def copy(src_id, dst_id, peer):
            src = own if src_id == 0 else store.at[src_id]
            return pltpu.make_async_remote_copy(
                src_ref=src,
                dst_ref=store.at[dst_id],
                send_sem=send.at[dst_id],
                recv_sem=recv.at[dst_id],
                device_id=peer,
                device_id_type=MESH,
            )

        copies = {}

        def start(src_id, dst_id, peer):
            copies[dst_id] = copy(src_id, dst_id, peer)
            copies[dst_id].start()

        def forward(dz, db):
            if db == 0:
                for d in range(1, side):
                    start(ident(dz, 0, 0), ident(dz, d, 0), ahead[1][d - 1])
            for d in range(1, side):
                start(ident(dz, db, 0), ident(dz, db, d), ahead[2][d - 1])

        def begin():
            for d in range(1, planes):
                start(0, d, ahead[0][d - 1])
            forward(0, 0)

        def arrive(dz, db, dc):
            copies[ident(dz, db, dc)].wait_recv()

        return begin, forward, arrive, copies

    p_begin, p_forward, p_arrive, p_copies = gather(pos_ref, pos_all, p_send, p_recv)
    f_begin, f_forward, f_arrive, f_copies = gather(masked_ref, feat_all, f_send, f_recv)

    def core_copy(src, dst, k):
        return pltpu.make_async_remote_copy(
            src_ref=src,
            dst_ref=dst,
            send_sem=c_send.at[k],
            recv_sem=c_recv.at[k],
            device_id=partner,
            device_id_type=MESH,
        )

    p_begin()
    wave_copy = core_copy(wave_ref, wave_other, 0)
    wave_copy.start()
    f_begin()
    pos_all[0] = pos_ref[...]
    feat_all[0] = masked_ref[...]
    mixing_t = mixing_ref[...].T
    wave_copy.wait_recv()

    block = min(kw, 128)

    def angles(dz, db, dc):
        k = ident(dz, db, dc)
        place = pos_all[k]
        columns = slice(k * rows, (k + 1) * rows)
        for half, ref in enumerate((wave_ref, wave_other)):

            def one(j, carry):
                r0 = pl.multiple_of(j * block, block)
                turns = jnp.dot(
                    ref[pl.ds(r0, block), :][:, :16], place, preferred_element_type=F32
                )
                r = turns - jnp.round(turns)
                zz = r * r
                s = r * horner(zz, SIN)
                co = horner(zz, COS)
                base = half * 2 * kw
                trig[pl.ds(base + r0, block), columns] = (1.0 - s * s).astype(BF)
                trig[pl.ds(base + kw + r0, block), columns] = (s * co).astype(BF)
                return carry

            lax.fori_loop(0, kw // block, one, 0)

    group_cols = planes * rows
    step = min(2 * kw, 256)

    def sums(g, lo, hi, first):
        columns = slice(g * group_cols, (g + 1) * group_cols)

        def one(j, carry):
            r0 = pl.multiple_of(lo + j * step, step)
            feats_g = feat_all[g * planes : (g + 1) * planes].reshape(group_cols, width)
            part = jnp.dot(
                trig[pl.ds(r0, step), columns], feats_g, preferred_element_type=F32
            )
            if first:
                factors[pl.ds(r0, step), :] = part
            else:
                factors[pl.ds(r0, step), :] += part
            return carry

        lax.fori_loop(0, (hi - lo) // step, one, 0)

    angles(0, 0, 0)
    for dz in range(1, planes):
        p_arrive(dz, 0, 0)
        p_forward(dz, 0)
    for dz in range(1, planes):
        angles(dz, 0, 0)
        f_arrive(dz, 0, 0)
        f_forward(dz, 0)
    for db in range(1, side):
        for dz in range(planes):
            p_arrive(dz, db, 0)
            p_forward(dz, db)
    for db in range(1, side):
        for dz in range(planes):
            angles(dz, db, 0)
            f_arrive(dz, db, 0)
            f_forward(dz, db)
    groups = side * side
    for g in range(side):
        if g < groups - 1:
            sums(g, 0, 4 * kw, g == 0)
    for dc in range(1, side):
        for db in range(side):
            for dz in range(planes):
                p_arrive(dz, db, dc)
                angles(dz, db, dc)
    for dc in range(1, side):
        for db in range(side):
            for dz in range(planes):
                f_arrive(dz, db, dc)
            g = dc * side + db
            if g < groups - 1:
                sums(g, 0, 4 * kw, False)
    last = groups - 1
    sums(last, 2 * kw, 4 * kw, last == 0)
    sum_copy = core_copy(factors.at[pl.ds(2 * kw, 2 * kw)], factors_in, 1)
    sum_copy.start()
    sums(last, 0, 2 * kw, last == 0)
    filt = filt_ref[...].astype(F32)
    scale = 1.0 / math.sqrt(atoms_all)
    sum_copy.wait_recv()
    for part in range(2):
        span = slice(part * kw, (part + 1) * kw)
        total = (factors[span, :] + factors_in[span, :]) * scale * filt
        field_t[:, span] = lax.dot_general(
            mixing_t, total, (((1,), (1,)), ((), ())), precision=HIGHEST,
            preferred_element_type=F32,
        ).astype(BF)
    field_copy = core_copy(field_t, field_other, 2)
    field_copy.start()
    field_copy.wait_recv()

    inv_k = 1.0 / math.sqrt(kwaves_all)

    def update_pair(k):
        columns = slice(k * rows, (k + 2) * rows)
        return jnp.dot(
            field_t[...], trig[: 2 * kw, columns], preferred_element_type=F32
        ) + jnp.dot(field_other[...], trig[2 * kw :, columns], preferred_element_type=F32)

    u_copies = {}

    def start_u(k, dst_id, peer):
        u_copies[dst_id] = pltpu.make_async_remote_copy(
            src_ref=send_u.at[k],
            dst_ref=recv_u.at[dst_id],
            send_sem=u_send.at[dst_id],
            recv_sem=u_recv.at[dst_id],
            device_id=peer,
            device_id_type=MESH,
        )
        u_copies[dst_id].start()

    def received(k):
        u_copies[k].wait_recv()
        return recv_u[k].astype(F32)

    order = [(dz, db) for db in range(side - 1, -1, -1) for dz in range(planes - 2, -1, -2)]
    for dz, db in order:
        for dc in range(1, side):
            k = ident(dz, db, dc)
            pair = update_pair(k)
            for d in range(2):
                send_u[k + d] = pair[:, d * rows : (d + 1) * rows].astype(BF)
                start_u(k + d, k + d, back[2][dc - 1])
    for dz, db in order:
        k = ident(dz, db, 0)
        pair = update_pair(k)
        for d in range(2):
            kept[k + d] = pair[:, d * rows : (d + 1) * rows]

    def collected(dz, db):
        acc = kept[ident(dz, db, 0)]
        for d in range(1, side):
            acc = acc + received(ident(dz, db, d))
        if db == 0:
            for d in range(1, side):
                acc = acc + received(ident(dz, d, 0))
        return acc

    zorder = [dz + d for dz in range(planes - 2, -1, -2) for d in range(2)]
    for db in range(side - 1, 0, -1):
        for dz in zorder:
            k = ident(dz, db, 0)
            send_u[k] = collected(dz, db).astype(BF)
            start_u(k, k, back[1][db - 1])
    for dz in zorder:
        if dz:
            send_u[dz] = collected(dz, 0).astype(BF)
            start_u(dz, dz, back[0][dz - 1])
    mine = collected(0, 0)
    for dz in range(1, planes):
        mine = mine + received(dz)

    state = masked_ref[...].astype(F32) + mine.T * inv_k
    meansq = jnp.mean(state * state, axis=1, keepdims=True)
    normed = (state * lax.rsqrt(meansq + 1e-06) * gain_ref[...]).astype(BF)
    inner = jnp.dot(normed, w_in_ref[...], preferred_element_type=F32)
    hidden = (inner / (1.0 + jnp.exp(-inner))).astype(BF)
    result = state + jnp.dot(hidden, w_out_ref[...], preferred_element_type=F32)
    slot = lax.broadcasted_iota(jnp.int32, (rows, width), 0)
    out_ref[...] = jnp.where(slot < counts_ref[0], result, 0.0).astype(BF)

    for copies in (p_copies, f_copies, u_copies):
        for copy in copies.values():
            copy.wait_send()
    for copy in (wave_copy, sum_copy, field_copy):
        copy.wait_send()


def body(n, cores, positions, counts, feats, waves, wave_filter, mixing, gain, w_in, w_out):
    rows, width = feats.shape
    planes, side = grid_of(n)
    kwaves_all = waves.shape[1] * cores
    kw = waves.shape[1] // n
    me = lax.axis_index("atom")
    live = lax.broadcasted_iota(jnp.int32, (rows, 1), 0) < counts[0]
    masked = feats * live.astype(BF)
    high = lax.reduce_precision(positions, 8, 7)
    rest = positions - high
    middle = lax.reduce_precision(rest, 8, 7)
    low = rest - middle
    pos = jnp.pad(jnp.concatenate([high, middle, low], 0).astype(BF), ((0, 7), (0, 0)))
    own = lax.dynamic_slice_in_dim(waves, me * kw, kw, 1).astype(BF).T
    wave = jnp.pad(jnp.concatenate([own, own, own], 1), ((0, 0), (0, 119)))
    filt = lax.dynamic_slice_in_dim(wave_filter, me * kw, kw, 0)
    vmem = pl.BlockSpec(memory_space=pltpu.VMEM)
    return pl.pallas_call(
        functools.partial(kernel, n, planes, side, rows * n * cores, kwaves_all),
        out_shape=jax.ShapeDtypeStruct((rows, width), BF),
        in_specs=[pl.BlockSpec(memory_space=pltpu.SMEM)] + [vmem] * 8,
        out_specs=vmem,
        scratch_shapes=[
            pltpu.VMEM((n, 16, rows), BF),
            pltpu.VMEM((n, rows, width), BF),
            pltpu.VMEM((kw, 128), BF),
            pltpu.VMEM((4 * kw, n * rows), BF),
            pltpu.VMEM((4 * kw, width), F32),
            pltpu.VMEM((2 * kw, width), F32),
            pltpu.VMEM((width, 2 * kw), BF),
            pltpu.VMEM((width, 2 * kw), BF),
            pltpu.VMEM((n // side, width, rows), F32),
            pltpu.VMEM((n, width, rows), BF),
            pltpu.VMEM((n, width, rows), BF),
        ]
        + [pltpu.SemaphoreType.DMA((n,))] * 6
        + [pltpu.SemaphoreType.DMA((3,))] * 2,
        compiler_params=pltpu.CompilerParams(
            collective_id=0, has_side_effects=True, vmem_limit_bytes=60 * 2**20
        ),
    )(counts, pos, masked, wave, filt, mixing, gain[None, :], w_in, w_out)


def solution(mesh):
    n, cores = mesh.shape["atom"], mesh.shape["wave"]
    return jax.shard_map(
        functools.partial(body, n, cores),
        mesh=mesh,
        in_specs=(
            P(None, ("atom", "wave")),
            P(("atom", "wave")),
            P(("atom", "wave"), None),
            P(None, "wave"),
            P("wave", None),
            P(),
            P(),
            P(),
            P(),
        ),
        out_specs=P(("atom", "wave"), None),
        check_vma=False,
    )
```

```python
import functools
import math

import jax
import jax.numpy as jnp
from jax import lax
from jax.experimental import pallas as pl
from jax.experimental.pallas import tpu as pltpu
from jax.sharding import PartitionSpec as P

MESH = pl.DeviceIdType.MESH
BF, F32 = jnp.bfloat16, jnp.float32
HIGHEST = lax.Precision.HIGHEST
SIN = (4.442883014678955, -7.308245658874512, 3.606354236602783, -0.8461116552352905, 0.1098245158791542)
COS = (1.4142135381698608, -6.978850841522217, 5.739460468292236, -1.883557915687561, 0.3106880187988281)


def horner(z, coefs):
    total = coefs[-1]
    for value in coefs[-2::-1]:
        total = total * z + value
    return total


def grid_of(n):
    side = 1
    while n % (4 * side * side) == 0 and 8 * side**3 <= n:
        side *= 2
    return n // (side * side), side


def kernel(
    n,
    planes,
    side,
    atoms_all,
    kwaves_all,
    counts_ref,
    pos_ref,
    feats_ref,
    waves_ref,
    filt_hbm,
    mixing_hbm,
    gain_ref,
    w_in_hbm,
    w_out_hbm,
    out_ref,
    filt_ref,
    mixing_ref,
    w_in_ref,
    w_out_ref,
    stage,
    wave_own,
    wave_raw,
    pos_all,
    feat_all,
    wave_other,
    trig,
    factors,
    factors_in,
    field_t,
    field_other,
    kept,
    send_u,
    recv_u,
    p_send,
    p_recv,
    f_send,
    f_recv,
    u_send,
    u_recv,
    c_send,
    c_recv,
    l_sem,
):
    kw, width = filt_ref.shape
    rows = feats_ref.shape[0]
    me = lax.axis_index("atom")
    core = lax.axis_index("wave")
    x = me % side
    y = (me // side) % side
    z = me // (side * side)
    b = y + core * (x - y)
    c = x + core * (y - x)
    stride_b = side + core * (1 - side)
    stride_c = 1 + core * (side - 1)

    def at(zz, bb, cc):
        return (zz * (side * side) + bb * stride_b + cc * stride_c, core)

    def ident(dz, db, dc):
        return (dc * side + db) * planes + dz

    partner = (me, 1 - core)
    ahead = (
        [at((z + d) % planes, b, c) for d in range(1, planes)],
        [at(z, (b + d) % side, c) for d in range(1, side)],
        [at(z, b, (c + d) % side) for d in range(1, side)],
    )
    back = (
        [at((z + planes - d) % planes, b, c) for d in range(1, planes)],
        [at(z, (b + side - d) % side, c) for d in range(1, side)],
        [at(z, b, (c + side - d) % side) for d in range(1, side)],
    )

    barrier = pltpu.get_barrier_semaphore()
    peers = [partner] + [peer for group in ahead for peer in group]
    for peer in peers:
        pl.semaphore_signal(barrier, inc=1, device_id=peer, device_id_type=MESH)

    local = [
        pltpu.make_async_copy(src, dst, l_sem.at[k])
        for k, (src, dst) in enumerate(
            (
                (mixing_hbm, mixing_ref),
                (filt_hbm.at[pl.ds(pl.multiple_of(me * kw, kw), kw)], filt_ref),
                (w_in_hbm, w_in_ref),
                (w_out_hbm, w_out_ref),
            )
        )
    ]
    for copy in local:
        copy.start()

    place = pos_ref[...]
    high = place.astype(BF).astype(F32)
    middle = (place - high).astype(BF).astype(F32)
    stage[...] = jnp.zeros_like(stage)
    stage[0:3, :rows] = high
    stage[3:6, :rows] = middle
    stage[6:9, :rows] = place - high - middle
    pos_all[0] = stage[:, :rows].astype(BF)
    slot = lax.broadcasted_iota(jnp.int32, (rows, width), 0)
    live = slot < counts_ref[0]
    feats = feats_ref[...].astype(F32)
    feat_all[0] = jnp.where(live, feats, 0.0).astype(BF)

    window = max(kw, 128)
    first = pl.multiple_of((me * kw) // window * window, window)
    shift = me * kw - first

    def turned(raw):
        for part in range(3):
            stage[3 * part : 3 * part + 3, :] = raw.astype(F32)
        found = stage[...]
        if kw < window:
            found = pltpu.roll(found, (window - shift) % window, 1)
        return found.T[:kw].astype(BF)

    pl.semaphore_wait(barrier, len(peers))

    def gather(store, send, recv):
        def copy(src_id, dst_id, peer):
            src = store.at[src_id]
            return pltpu.make_async_remote_copy(
                src_ref=src,
                dst_ref=store.at[dst_id],
                send_sem=send.at[dst_id],
                recv_sem=recv.at[dst_id],
                device_id=peer,
                device_id_type=MESH,
            )

        copies = {}

        def start(src_id, dst_id, peer):
            copies[dst_id] = copy(src_id, dst_id, peer)
            copies[dst_id].start()

        def forward(dz, db):
            if db == 0:
                for d in range(1, side):
                    start(ident(dz, 0, 0), ident(dz, d, 0), ahead[1][d - 1])
            for d in range(1, side):
                start(ident(dz, db, 0), ident(dz, db, d), ahead[2][d - 1])

        def begin():
            for d in range(1, planes):
                start(0, d, ahead[0][d - 1])
            forward(0, 0)

        def arrive(dz, db, dc):
            copies[ident(dz, db, dc)].wait_recv()

        return begin, forward, arrive, copies

    p_begin, p_forward, p_arrive, p_copies = gather(pos_all, p_send, p_recv)
    f_begin, f_forward, f_arrive, f_copies = gather(feat_all, f_send, f_recv)

    def core_copy(src, dst, k):
        return pltpu.make_async_remote_copy(
            src_ref=src,
            dst_ref=dst,
            send_sem=c_send.at[k],
            recv_sem=c_recv.at[k],
            device_id=partner,
            device_id_type=MESH,
        )

    p_begin()
    wave_copy = core_copy(waves_ref.at[:, pl.ds(first, window)], wave_raw, 0)
    wave_copy.start()
    f_begin()
    wave_own[...] = turned(waves_ref[:, pl.ds(first, window)])
    wave_copy.wait_recv()
    wave_other[...] = turned(wave_raw[...])

    block = min(kw, 128)

    def angles(dz, db, dc):
        k = ident(dz, db, dc)
        place = pos_all[k]
        columns = slice(k * rows, (k + 1) * rows)
        for half, ref in enumerate((wave_own, wave_other)):

            def one(j, carry):
                r0 = pl.multiple_of(j * block, block)
                turns = jnp.dot(
                    ref[pl.ds(r0, block), :], place, preferred_element_type=F32
                )
                r = turns - jnp.round(turns)
                zz = r * r
                s = r * horner(zz, SIN)
                co = horner(zz, COS)
                base = half * 2 * kw
                trig[pl.ds(base + r0, block), columns] = (1.0 - s * s).astype(BF)
                trig[pl.ds(base + kw + r0, block), columns] = (s * co).astype(BF)
                return carry

            lax.fori_loop(0, kw // block, one, 0)

    group_cols = planes * rows
    step = min(2 * kw, 256)

    def sums(g, lo, hi, first):
        columns = slice(g * group_cols, (g + 1) * group_cols)

        def one(j, carry):
            r0 = pl.multiple_of(lo + j * step, step)
            feats_g = feat_all[g * planes : (g + 1) * planes].reshape(group_cols, width)
            part = jnp.dot(
                trig[pl.ds(r0, step), columns], feats_g, preferred_element_type=F32
            )
            if first:
                factors[pl.ds(r0, step), :] = part
            else:
                factors[pl.ds(r0, step), :] += part
            return carry

        lax.fori_loop(0, (hi - lo) // step, one, 0)

    angles(0, 0, 0)
    for dz in range(1, planes):
        p_arrive(dz, 0, 0)
        p_forward(dz, 0)
    for dz in range(1, planes):
        angles(dz, 0, 0)
        f_arrive(dz, 0, 0)
        f_forward(dz, 0)
    for db in range(1, side):
        for dz in range(planes):
            p_arrive(dz, db, 0)
            p_forward(dz, db)
    for db in range(1, side):
        for dz in range(planes):
            angles(dz, db, 0)
            f_arrive(dz, db, 0)
            f_forward(dz, db)
    groups = side * side
    for g in range(side):
        if g < groups - 1:
            sums(g, 0, 4 * kw, g == 0)
    for dc in range(1, side):
        for db in range(side):
            for dz in range(planes):
                p_arrive(dz, db, dc)
                angles(dz, db, dc)
    for dc in range(1, side):
        for db in range(side):
            for dz in range(planes):
                f_arrive(dz, db, dc)
            g = dc * side + db
            if g < groups - 1:
                sums(g, 0, 4 * kw, False)
    last = groups - 1
    sums(last, 2 * kw, 4 * kw, last == 0)
    sum_copy = core_copy(factors.at[pl.ds(2 * kw, 2 * kw)], factors_in, 1)
    sum_copy.start()
    sums(last, 0, 2 * kw, last == 0)
    for copy in local:
        copy.wait()
    mixing_t = mixing_ref[...].T
    filt = filt_ref[...].astype(F32)
    scale = 1.0 / math.sqrt(atoms_all)
    sum_copy.wait_recv()
    for part in range(2):
        span = slice(part * kw, (part + 1) * kw)
        total = (factors[span, :] + factors_in[span, :]) * scale * filt
        field_t[:, span] = lax.dot_general(
            mixing_t, total, (((1,), (1,)), ((), ())), precision=HIGHEST,
            preferred_element_type=F32,
        ).astype(BF)
    field_copy = core_copy(field_t, field_other, 2)
    field_copy.start()
    field_copy.wait_recv()

    inv_k = 1.0 / math.sqrt(kwaves_all)

    def update_pair(k):
        columns = slice(k * rows, (k + 2) * rows)
        return jnp.dot(
            field_t[...], trig[: 2 * kw, columns], preferred_element_type=F32
        ) + jnp.dot(field_other[...], trig[2 * kw :, columns], preferred_element_type=F32)

    u_copies = {}

    def start_u(k, dst_id, peer):
        u_copies[dst_id] = pltpu.make_async_remote_copy(
            src_ref=send_u.at[k],
            dst_ref=recv_u.at[dst_id],
            send_sem=u_send.at[dst_id],
            recv_sem=u_recv.at[dst_id],
            device_id=peer,
            device_id_type=MESH,
        )
        u_copies[dst_id].start()

    def received(k):
        u_copies[k].wait_recv()
        return recv_u[k].astype(F32)

    order = [(dz, db) for db in range(side - 1, -1, -1) for dz in range(planes - 2, -1, -2)]
    for dz, db in order:
        for dc in range(1, side):
            k = ident(dz, db, dc)
            pair = update_pair(k)
            for d in range(2):
                send_u[k + d] = pair[:, d * rows : (d + 1) * rows].astype(BF)
                start_u(k + d, k + d, back[2][dc - 1])
    for dz, db in order:
        k = ident(dz, db, 0)
        pair = update_pair(k)
        for d in range(2):
            kept[k + d] = pair[:, d * rows : (d + 1) * rows]

    def collected(dz, db):
        acc = kept[ident(dz, db, 0)]
        for d in range(1, side):
            acc = acc + received(ident(dz, db, d))
        if db == 0:
            for d in range(1, side):
                acc = acc + received(ident(dz, d, 0))
        return acc

    zorder = [dz + d for dz in range(planes - 2, -1, -2) for d in range(2)]
    for db in range(side - 1, 0, -1):
        for dz in zorder:
            k = ident(dz, db, 0)
            send_u[k] = collected(dz, db).astype(BF)
            start_u(k, k, back[1][db - 1])
    for dz in zorder:
        if dz:
            send_u[dz] = collected(dz, 0).astype(BF)
            start_u(dz, dz, back[0][dz - 1])
    mine = collected(0, 0)
    for dz in range(1, planes):
        mine = mine + received(dz)

    state = feats + mine.T * inv_k
    meansq = jnp.mean(state * state, axis=1, keepdims=True)
    normed = (state * lax.rsqrt(meansq + 1e-06) * gain_ref[...].reshape(1, width)).astype(BF)
    inner = jnp.dot(normed, w_in_ref[...], preferred_element_type=F32)
    hidden = (inner / (1.0 + jnp.exp(-inner))).astype(BF)
    result = state + jnp.dot(hidden, w_out_ref[...], preferred_element_type=F32)
    out_ref[...] = jnp.where(live, result, 0.0)

    for copies in (p_copies, f_copies, u_copies):
        for copy in copies.values():
            copy.wait_send()
    for copy in (wave_copy, sum_copy, field_copy):
        copy.wait_send()


def body(n, cores, positions, counts, feats, waves, wave_filter, mixing, gain, w_in, w_out):
    rows, width = feats.shape
    planes, side = grid_of(n)
    kwaves_all = waves.shape[1] * cores
    kw = waves.shape[1] // n
    vmem = pl.BlockSpec(memory_space=pltpu.VMEM)
    hbm = pl.BlockSpec(memory_space=pl.ANY)
    return pl.pallas_call(
        functools.partial(kernel, n, planes, side, rows * n * cores, kwaves_all),
        out_shape=jax.ShapeDtypeStruct((rows, width), F32),
        in_specs=[pl.BlockSpec(memory_space=pltpu.SMEM)]
        + [vmem] * 3
        + [hbm] * 2
        + [vmem]
        + [hbm] * 2,
        out_specs=vmem,
        scratch_shapes=[
            pltpu.VMEM((kw, width), BF),
            pltpu.VMEM(mixing.shape, F32),
            pltpu.VMEM(w_in.shape, BF),
            pltpu.VMEM(w_out.shape, BF),
            pltpu.VMEM((16, max(kw, 128)), F32),
            pltpu.VMEM((kw, 16), BF),
            pltpu.VMEM((3, max(kw, 128)), waves.dtype),
            pltpu.VMEM((n, 16, rows), BF),
            pltpu.VMEM((n, rows, width), BF),
            pltpu.VMEM((kw, 16), BF),
            pltpu.VMEM((4 * kw, n * rows), BF),
            pltpu.VMEM((4 * kw, width), F32),
            pltpu.VMEM((2 * kw, width), F32),
            pltpu.VMEM((width, 2 * kw), BF),
            pltpu.VMEM((width, 2 * kw), BF),
            pltpu.VMEM((n // side, width, rows), F32),
            pltpu.VMEM((n, width, rows), BF),
            pltpu.VMEM((n, width, rows), BF),
        ]
        + [pltpu.SemaphoreType.DMA((n,))] * 6
        + [pltpu.SemaphoreType.DMA((3,))] * 2
        + [pltpu.SemaphoreType.DMA((4,))],
        compiler_params=pltpu.CompilerParams(
            collective_id=0, has_side_effects=True, vmem_limit_bytes=60 * 2**20
        ),
    )(counts, positions, feats, waves, wave_filter, mixing, gain, w_in, w_out).astype(BF)


def solution(mesh):
    n, cores = mesh.shape["atom"], mesh.shape["wave"]
    return jax.shard_map(
        functools.partial(body, n, cores),
        mesh=mesh,
        in_specs=(
            P(None, ("atom", "wave")),
            P(("atom", "wave")),
            P(("atom", "wave"), None),
            P(None, "wave"),
            P("wave", None),
            P(),
            P(),
            P(),
            P(),
        ),
        out_specs=P(("atom", "wave"), None),
        check_vma=False,
    )
```

```python
import functools
import math

import jax
import jax.numpy as jnp
from jax import lax
from jax.experimental import pallas as pl
from jax.experimental.pallas import tpu as pltpu
from jax.sharding import PartitionSpec as P

MESH = pl.DeviceIdType.MESH
BF, F32 = jnp.bfloat16, jnp.float32
HIGHEST = lax.Precision.HIGHEST
SIN = (4.442883014678955, -7.308245658874512, 3.606354236602783, -0.8461116552352905, 0.1098245158791542)
COS = (1.4142135381698608, -6.978850841522217, 5.739460468292236, -1.883557915687561, 0.3106880187988281)


def horner(z, coefs):
    total = coefs[-1]
    for value in coefs[-2::-1]:
        total = total * z + value
    return total


def grid_of(n):
    side = 1
    while n % (4 * side * side) == 0 and 8 * side**3 <= n:
        side *= 2
    return n // (side * side), side


def kernel(
    n,
    planes,
    side,
    atoms_all,
    kwaves_all,
    counts_ref,
    pos_ref,
    feats_ref,
    waves_ref,
    filt_hbm,
    mixing_hbm,
    gain_ref,
    w_in_hbm,
    w_out_hbm,
    out_ref,
    filt_ref,
    mixing_ref,
    w_in_ref,
    w_out_ref,
    stage,
    wave_own,
    wave_raw,
    pos_all,
    feat_all,
    wave_other,
    trig,
    factors,
    factors_in,
    field_t,
    field_other,
    kept,
    send_u,
    recv_u,
    p_send,
    p_recv,
    f_send,
    f_recv,
    u_send,
    u_recv,
    c_send,
    c_recv,
    l_sem,
):
    kw, width = filt_ref.shape
    rows = feats_ref.shape[0]
    me = lax.axis_index("atom")
    core = lax.axis_index("wave")
    x = me % side
    y = (me // side) % side
    z = me // (side * side)
    b = y + core * (x - y)
    c = x + core * (y - x)
    stride_b = side + core * (1 - side)
    stride_c = 1 + core * (side - 1)

    def at(zz, bb, cc):
        return (zz * (side * side) + bb * stride_b + cc * stride_c, core)

    def ident(dz, db, dc):
        return (dc * side + db) * planes + dz

    partner = (me, 1 - core)
    ahead = (
        [at((z + d) % planes, b, c) for d in range(1, planes)],
        [at(z, (b + d) % side, c) for d in range(1, side)],
        [at(z, b, (c + d) % side) for d in range(1, side)],
    )
    back = (
        [at((z + planes - d) % planes, b, c) for d in range(1, planes)],
        [at(z, (b + side - d) % side, c) for d in range(1, side)],
        [at(z, b, (c + side - d) % side) for d in range(1, side)],
    )

    barrier = pltpu.get_barrier_semaphore()
    peers = [partner] + [peer for group in ahead for peer in group]
    for peer in peers:
        pl.semaphore_signal(barrier, inc=1, device_id=peer, device_id_type=MESH)

    local = [
        pltpu.make_async_copy(src, dst, l_sem.at[k])
        for k, (src, dst) in enumerate(
            (
                (mixing_hbm, mixing_ref),
                (filt_hbm.at[pl.ds(pl.multiple_of(me * kw, kw), kw)], filt_ref),
                (w_in_hbm, w_in_ref),
                (w_out_hbm, w_out_ref),
            )
        )
    ]
    for copy in local:
        copy.start()

    place = pos_ref[...]
    high = place.astype(BF).astype(F32)
    middle = (place - high).astype(BF).astype(F32)
    stage[...] = jnp.zeros_like(stage)
    stage[0:3, :rows] = high
    stage[3:6, :rows] = middle
    stage[6:9, :rows] = place - high - middle
    pos_all[0] = stage[:, :rows].astype(BF)
    slot = lax.broadcasted_iota(jnp.int32, (rows, width), 0)
    live = slot < counts_ref[0]
    feats = feats_ref[...].astype(F32)
    feat_all[0] = jnp.where(live, feats, 0.0).astype(BF)

    window = max(kw, 128)
    first = pl.multiple_of((me * kw) // window * window, window)
    shift = me * kw - first

    def turned(raw):
        for part in range(3):
            stage[3 * part : 3 * part + 3, :] = raw.astype(F32)
        found = stage[...]
        if kw < window:
            found = pltpu.roll(found, (window - shift) % window, 1)
        return found.T[:kw].astype(BF)

    pl.semaphore_wait(barrier, len(peers))

    def gather(store, send, recv):
        def copy(src_id, dst_id, peer):
            src = store.at[src_id]
            return pltpu.make_async_remote_copy(
                src_ref=src,
                dst_ref=store.at[dst_id],
                send_sem=send.at[dst_id],
                recv_sem=recv.at[dst_id],
                device_id=peer,
                device_id_type=MESH,
            )

        copies = {}

        def start(src_id, dst_id, peer):
            copies[dst_id] = copy(src_id, dst_id, peer)
            copies[dst_id].start()

        def forward(dz, db):
            if db == 0:
                for d in range(1, side):
                    start(ident(dz, 0, 0), ident(dz, d, 0), ahead[1][d - 1])
            for d in range(1, side):
                start(ident(dz, db, 0), ident(dz, db, d), ahead[2][d - 1])

        def begin():
            for d in range(1, planes):
                start(0, d, ahead[0][d - 1])
            forward(0, 0)

        def arrive(dz, db, dc):
            copies[ident(dz, db, dc)].wait_recv()

        return begin, forward, arrive, copies

    p_begin, p_forward, p_arrive, p_copies = gather(pos_all, p_send, p_recv)
    f_begin, f_forward, f_arrive, f_copies = gather(feat_all, f_send, f_recv)

    def core_copy(src, dst, k):
        return pltpu.make_async_remote_copy(
            src_ref=src,
            dst_ref=dst,
            send_sem=c_send.at[k],
            recv_sem=c_recv.at[k],
            device_id=partner,
            device_id_type=MESH,
        )

    p_begin()
    wave_copy = core_copy(waves_ref.at[:, pl.ds(first, window)], wave_raw, 0)
    wave_copy.start()
    f_begin()
    wave_own[...] = turned(waves_ref[:, pl.ds(first, window)])
    wave_copy.wait_recv()
    wave_other[...] = turned(wave_raw[...])

    block = min(kw, 128)

    def angles(dz, db, dc):
        k = ident(dz, db, dc)
        place = pos_all[k]
        columns = slice(k * rows, (k + 1) * rows)
        for half, ref in enumerate((wave_own, wave_other)):

            def one(j, carry):
                r0 = pl.multiple_of(j * block, block)
                turns = jnp.dot(
                    ref[pl.ds(r0, block), :], place, preferred_element_type=F32
                )
                r = turns - jnp.round(turns)
                zz = r * r
                s = r * horner(zz, SIN)
                co = horner(zz, COS)
                base = half * 2 * kw
                trig[pl.ds(base + r0, block), columns] = (1.0 - s * s).astype(BF)
                trig[pl.ds(base + kw + r0, block), columns] = (s * co).astype(BF)
                return carry

            lax.fori_loop(0, kw // block, one, 0)

    group_cols = planes * rows
    step = min(kw, 256)

    def sums(g, lo, hi, first):
        columns = slice(g * group_cols, (g + 1) * group_cols)

        def one(j, carry):
            r0 = pl.multiple_of(lo + j * step, step)
            feats_g = feat_all[g * planes : (g + 1) * planes].reshape(group_cols, width)
            part = jnp.dot(
                trig[pl.ds(r0, step), columns], feats_g, preferred_element_type=F32
            )
            if first:
                factors[pl.ds(r0, step), :] = part
            else:
                factors[pl.ds(r0, step), :] += part
            return carry

        lax.fori_loop(0, (hi - lo) // step, one, 0)

    groups = side * side
    near = range(1, side)
    far = range(1, planes)

    def group_sums(dc, db):
        g = dc * side + db
        if g < groups - 1:
            sums(g, 0, 4 * kw, g == 0)

    angles(0, 0, 0)
    for dz in far:
        p_arrive(dz, 0, 0)
        p_forward(dz, 0)
    for db in near:
        p_arrive(0, db, 0)
        p_forward(0, db)
        f_arrive(0, db, 0)
        f_forward(0, db)
        angles(0, db, 0)
    for dz in far:
        f_arrive(dz, 0, 0)
        f_forward(dz, 0)
        for db in near:
            p_arrive(dz, db, 0)
            p_forward(dz, db)
        angles(dz, 0, 0)
    for dz in far:
        for db in near:
            angles(dz, db, 0)
            f_arrive(dz, db, 0)
            f_forward(dz, db)
    for dc in near:
        for db in range(side):
            for dz in range(planes):
                p_arrive(dz, db, dc)
                angles(dz, db, dc)
            if dc == 1:
                group_sums(0, db)
    for dc in near:
        for db in range(side):
            for dz in range(planes):
                f_arrive(dz, db, dc)
            group_sums(dc, db)
    last = groups - 1
    sum_copies = []
    for part in range(2):
        sums(last, (2 + part) * kw, (3 + part) * kw, last == 0)
        sum_copies.append(
            core_copy(
                factors.at[pl.ds((2 + part) * kw, kw)],
                factors_in.at[pl.ds(part * kw, kw)],
                (1, 3)[part],
            )
        )
        sum_copies[part].start()
    sums(last, 0, 2 * kw, last == 0)
    for copy in local:
        copy.wait()
    mixing_t = mixing_ref[...].T
    filt = filt_ref[...].astype(F32)
    scale = 1.0 / math.sqrt(atoms_all)
    for part in range(2):
        sum_copies[part].wait_recv()
        span = slice(part * kw, (part + 1) * kw)
        total = (factors[span, :] + factors_in[span, :]) * scale * filt
        field_t[:, span] = lax.dot_general(
            mixing_t, total, (((1,), (1,)), ((), ())), precision=HIGHEST,
            preferred_element_type=F32,
        ).astype(BF)
    field_copy = core_copy(field_t, field_other, 2)
    field_copy.start()
    field_copy.wait_recv()

    inv_k = 1.0 / math.sqrt(kwaves_all)

    def update_pair(k):
        columns = slice(k * rows, (k + 2) * rows)
        return jnp.dot(
            field_t[...], trig[: 2 * kw, columns], preferred_element_type=F32
        ) + jnp.dot(field_other[...], trig[2 * kw :, columns], preferred_element_type=F32)

    u_copies = {}

    def start_u(k, dst_id, peer):
        u_copies[dst_id] = pltpu.make_async_remote_copy(
            src_ref=send_u.at[k],
            dst_ref=recv_u.at[dst_id],
            send_sem=u_send.at[dst_id],
            recv_sem=u_recv.at[dst_id],
            device_id=peer,
            device_id_type=MESH,
        )
        u_copies[dst_id].start()

    def received(k):
        u_copies[k].wait_recv()
        return recv_u[k].astype(F32)

    def push(pair, k, dz, dc):
        for d in range(2):
            send_u[k + d] = pair[:, d * rows : (d + 1) * rows].astype(BF)
            if dz + d:
                start_u(k + d, k + d, back[2][dc - 1])

    order = [
        (dz, db) for dz in range(planes - 2, -1, -2) for db in range(side - 1, -1, -1)
    ]
    for dz, db in order:
        for dc in near:
            k = ident(dz, db, dc)
            push(update_pair(k), k, dz, dc)
    for db in range(side - 1, -1, -1):
        for dc in near:
            k = ident(0, db, dc)
            start_u(k, k, back[2][dc - 1])
    for dz, db in order:
        k = ident(dz, db, 0)
        pair = update_pair(k)
        for d in range(2):
            kept[k + d] = pair[:, d * rows : (d + 1) * rows]

    def collected(dz, db):
        acc = kept[ident(dz, db, 0)]
        for d in range(1, side):
            acc = acc + received(ident(dz, db, d))
        if db == 0:
            for d in range(1, side):
                acc = acc + received(ident(dz, d, 0))
        return acc

    def pass_b(dz):
        for db in near:
            k = ident(dz, db, 0)
            send_u[k] = collected(dz, db).astype(BF)
            start_u(k, k, back[1][db - 1])

    def pass_a(dz):
        send_u[dz] = collected(dz, 0).astype(BF)
        start_u(dz, dz, back[0][dz - 1])

    zorder = [dz + d for dz in range(planes - 2, -1, -2) for d in range(2) if dz + d]
    for dz in zorder:
        pass_b(dz)
    for dz in zorder[:-1]:
        pass_a(dz)
    pass_b(0)
    if zorder:
        pass_a(zorder[-1])
    mine = collected(0, 0)
    for dz in range(1, planes):
        mine = mine + received(dz)

    state = feats + mine.T * inv_k
    meansq = jnp.mean(state * state, axis=1, keepdims=True)
    normed = (state * lax.rsqrt(meansq + 1e-06) * gain_ref[...].reshape(1, width)).astype(BF)
    inner = jnp.dot(normed, w_in_ref[...], preferred_element_type=F32)
    hidden = (inner / (1.0 + jnp.exp(-inner))).astype(BF)
    result = state + jnp.dot(hidden, w_out_ref[...], preferred_element_type=F32)
    out_ref[...] = jnp.where(live, result, 0.0)

    for copies in (p_copies, f_copies, u_copies):
        for copy in copies.values():
            copy.wait_send()
    for copy in (wave_copy, *sum_copies, field_copy):
        copy.wait_send()


def body(n, cores, positions, counts, feats, waves, wave_filter, mixing, gain, w_in, w_out):
    rows, width = feats.shape
    planes, side = grid_of(n)
    kwaves_all = waves.shape[1] * cores
    kw = waves.shape[1] // n
    vmem = pl.BlockSpec(memory_space=pltpu.VMEM)
    hbm = pl.BlockSpec(memory_space=pl.ANY)
    return pl.pallas_call(
        functools.partial(kernel, n, planes, side, rows * n * cores, kwaves_all),
        out_shape=jax.ShapeDtypeStruct((rows, width), F32),
        in_specs=[pl.BlockSpec(memory_space=pltpu.SMEM)]
        + [vmem] * 3
        + [hbm] * 2
        + [vmem]
        + [hbm] * 2,
        out_specs=vmem,
        scratch_shapes=[
            pltpu.VMEM((kw, width), BF),
            pltpu.VMEM(mixing.shape, F32),
            pltpu.VMEM(w_in.shape, BF),
            pltpu.VMEM(w_out.shape, BF),
            pltpu.VMEM((16, max(kw, 128)), F32),
            pltpu.VMEM((kw, 16), BF),
            pltpu.VMEM((3, max(kw, 128)), waves.dtype),
            pltpu.VMEM((n, 16, rows), BF),
            pltpu.VMEM((n, rows, width), BF),
            pltpu.VMEM((kw, 16), BF),
            pltpu.VMEM((4 * kw, n * rows), BF),
            pltpu.VMEM((4 * kw, width), F32),
            pltpu.VMEM((2 * kw, width), F32),
            pltpu.VMEM((width, 2 * kw), BF),
            pltpu.VMEM((width, 2 * kw), BF),
            pltpu.VMEM((n // side, width, rows), F32),
            pltpu.VMEM((n, width, rows), BF),
            pltpu.VMEM((n, width, rows), BF),
        ]
        + [pltpu.SemaphoreType.DMA((n,))] * 6
        + [pltpu.SemaphoreType.DMA((4,))] * 2
        + [pltpu.SemaphoreType.DMA((4,))],
        compiler_params=pltpu.CompilerParams(
            collective_id=0, has_side_effects=True, vmem_limit_bytes=60 * 2**20
        ),
    )(counts, positions, feats, waves, wave_filter, mixing, gain, w_in, w_out).astype(BF)


def solution(mesh):
    n, cores = mesh.shape["atom"], mesh.shape["wave"]
    return jax.shard_map(
        functools.partial(body, n, cores),
        mesh=mesh,
        in_specs=(
            P(None, ("atom", "wave")),
            P(("atom", "wave")),
            P(("atom", "wave"), None),
            P(None, "wave"),
            P("wave", None),
            P(),
            P(),
            P(),
            P(),
        ),
        out_specs=P(("atom", "wave"), None),
        check_vma=False,
    )
```
